32 devices in a mesh: section: 4 (over z), rows: 8 (over y, x, core).
Axes of the slice: x: 2, y: 2, z: 4, core: 2. Of those that a mesh axis runs over, the one named last changes fastest.
Arguments:
- top_values: float32 [4, 2, 256, 512], P(None, None, 'rows'), may hold values from -6 to 6
- top_cotangents: float32 [4, 2, 256, 512], P(None, None, 'rows'), may hold values from -6 to 6
- f_input: bfloat16 [4, 512, 256], P('section', 'rows'), may hold values from -0.25 to 0.25
- f_kernel: bfloat16 [4, 2304, 256], P('section', 'rows'), may hold values from -0.125 to 0.125
- f_output: bfloat16 [4, 256, 512], P('section', 'rows'), may hold values from -0.1875 to 0.1875
- g_input: bfloat16 [4, 512, 256], P('section', 'rows'), may hold values from -0.25 to 0.25
- g_kernel: bfloat16 [4, 2304, 256], P('section', 'rows'), may hold values from -0.125 to 0.125
- g_output: bfloat16 [4, 256, 512], P('section', 'rows'), may hold values from -0.1875 to 0.1875
Outputs:
- rebuilt: float32 [4, 4, 2, 256, 512], P('section', None, None, 'rows')
- cotangents: float32 [4, 4, 2, 256, 512], P('section', None, None, 'rows')
- grad_f_input: float32 [4, 512, 256], P('section', 'rows')
- grad_f_kernel: float32 [4, 2304, 256], P('section', 'rows')
- grad_f_output: float32 [4, 256, 512], P('section', 'rows')
- grad_g_input: float32 [4, 512, 256], P('section', 'rows')
- grad_g_kernel: float32 [4, 2304, 256], P('section', 'rows')
- grad_g_output: float32 [4, 256, 512], P('section', 'rows')
The draws below stay inside these ranges and needn't reach their ends.
All inputs are finite; a program needn't handle non-finite values.
Results may differ from the reference program's by a relative error of at most 0.034.
Values may be sent and summed in bfloat16 or wider, within the bound.
No kernel may reach another device: no remote copies, remote signals or barrier semaphores. Data moves between devices by JAX's collectives and lax.ppermute only.
A program may use at most 64 MiB of HBM per device.

```python
import jax
import jax.numpy as jnp
from jax import lax

HALF = 512
RANK = 256
ROWS_DEV = 4
COLS = 8
MICRO = 4
PIX = 256
N_SECTION = 4
N_ROWS = 8


def shard_levels(key, dims, cuts, smallest, largest):
    def one(dim, parts):
        heights = jax.random.uniform(jax.random.fold_in(jax.random.fold_in(key, 6), dim), (parts,), jnp.float32, smallest / len(cuts), largest / len(cuts))
        return jnp.repeat(jnp.exp(heights), dims[dim] // parts).reshape((-1,) + (1,) * (len(dims) - dim - 1))

    level = one(*cuts[0])
    for cut in cuts[1:]:
        level = level * one(*cut)
    return level


def scatter_about(rng, extent, spread, limit, cuts=(), dtype=jnp.bfloat16):
    level = shard_levels(rng, extent, cuts, -0.22, 0.18) if cuts else 1.0
    result = jax.random.normal(rng, extent, jnp.float32) * spread * level
    return jnp.minimum(jnp.maximum(result, -limit), limit).astype(dtype)


def setup_inputs(seed: int = 0) -> dict:
    arg_keys = jax.random.split(jax.random.key(seed), 9)
    return {
        "top_values": scatter_about(arg_keys[0], (MICRO, 2, PIX, HALF), 1.0, 6.0, ((2, 8),), jnp.float32),
        "top_cotangents": scatter_about(arg_keys[1], (MICRO, 2, PIX, HALF), 1.0, 6.0, ((2, 8),), jnp.float32),
        "f_input": scatter_about(arg_keys[2], (N_SECTION, HALF, RANK), HALF ** -0.5, 0.25, ((0, 4), (1, 8))),
        "f_kernel": scatter_about(arg_keys[3], (N_SECTION, 9 * RANK, RANK), (9 * RANK) ** -0.5, 0.125, ((0, 4), (1, 8))),
        "f_output": scatter_about(arg_keys[4], (N_SECTION, RANK, HALF), (4 * RANK) ** -0.5, 0.1875, ((0, 4), (1, 8))),
        "g_input": scatter_about(arg_keys[5], (N_SECTION, HALF, RANK), HALF ** -0.5, 0.25, ((0, 4), (1, 8))),
        "g_kernel": scatter_about(arg_keys[6], (N_SECTION, 9 * RANK, RANK), (9 * RANK) ** -0.5, 0.125, ((0, 4), (1, 8))),
        "g_output": scatter_about(arg_keys[7], (N_SECTION, RANK, HALF), (4 * RANK) ** -0.5, 0.1875, ((0, 4), (1, 8))),
    }


LOSS_SCALE = 32.0


def silu_slope(values):
    sigma_part = jax.nn.sigmoid(values)
    return sigma_part * (1.0 + values * (1.0 - sigma_part))


def matmul(left, right):
    return jnp.dot(left, right, preferred_element_type=jnp.float32)


def image_taps(hidden):
    channels = hidden.shape[1]
    height = ROWS_DEV * N_ROWS
    images = hidden.reshape(MICRO, height, COLS, channels)
    padded = jnp.pad(images, ((0, 0), (1, 1), (1, 1), (0, 0)))
    pieces = []
    for row_step in (-1, 0, 1):
        for col_step in (-1, 0, 1):
            pieces.append(padded[:, 1 + row_step:1 + row_step + height, 1 + col_step:1 + col_step + COLS, :])
    return jnp.concatenate(pieces, axis=3).reshape(MICRO * height * COLS, 9 * channels)


def flipped(kernel):
    rank_size = kernel.shape[1]
    return jnp.transpose(kernel.reshape(9, rank_size, rank_size)[::-1], (0, 2, 1)).reshape(9 * rank_size, rank_size)


def device_partial(left, right):
    left_part = left.astype(jnp.float32).reshape(MICRO, N_ROWS, -1, left.shape[1])
    right_part = right.astype(jnp.float32).reshape(MICRO, N_ROWS, -1, right.shape[1])
    partial_value = jnp.einsum("mrpa,mrpb->rab", left_part, right_part, precision=lax.Precision.HIGHEST)
    rounded = lax.optimization_barrier(partial_value.astype(jnp.bfloat16))
    return jnp.sum(rounded.astype(jnp.float32), axis=0) / LOSS_SCALE


def reference(top_values, top_cotangents, f_input, f_kernel, f_output, g_input, g_kernel, g_output):
    values_y1 = top_values[:, 0].reshape(-1, HALF)
    values_y2 = top_values[:, 1].reshape(-1, HALF)
    cot_y1 = top_cotangents[:, 0].reshape(-1, HALF)
    cot_y2 = top_cotangents[:, 1].reshape(-1, HALF)
    rebuilt_list = []
    cot_list = []
    grad_lists = [[], [], [], [], [], []]
    for section_index in range(N_SECTION - 1, -1, -1):
        w_f_in = f_input[section_index]
        w_f_core = f_kernel[section_index]
        w_f_out = f_output[section_index]
        w_g_in = g_input[section_index]
        w_g_core = g_kernel[section_index]
        w_g_out = g_output[section_index]
        hidden_g = matmul(values_y1.astype(jnp.bfloat16), w_g_in).astype(jnp.bfloat16)
        taps_g = image_taps(hidden_g)
        conv_g = matmul(taps_g, w_g_core)
        act_g = jax.nn.silu(conv_g).astype(jnp.bfloat16)
        values_x2 = values_y2 - matmul(act_g, w_g_out)
        rounded_x2 = values_x2.astype(jnp.bfloat16)
        hidden_f = matmul(rounded_x2, w_f_in).astype(jnp.bfloat16)
        taps_f = image_taps(hidden_f)
        conv_f = matmul(taps_f, w_f_core)
        act_f = jax.nn.silu(conv_f).astype(jnp.bfloat16)
        values_x1 = values_y1 - matmul(act_f, w_f_out)
        rounded_dy2 = cot_y2.astype(jnp.bfloat16)
        grad_conv_g = (matmul(rounded_dy2, w_g_out.T) * silu_slope(conv_g)).astype(jnp.bfloat16)
        grad_hidden_g = matmul(image_taps(grad_conv_g), flipped(w_g_core)).astype(jnp.bfloat16)
        cot_x1 = cot_y1 + matmul(grad_hidden_g, w_g_in.T)
        rounded_dx1 = cot_x1.astype(jnp.bfloat16)
        grad_conv_f = (matmul(rounded_dx1, w_f_out.T) * silu_slope(conv_f)).astype(jnp.bfloat16)
        grad_hidden_f = matmul(image_taps(grad_conv_f), flipped(w_f_core)).astype(jnp.bfloat16)
        cot_x2 = cot_y2 + matmul(grad_hidden_f, w_f_in.T)
        grad_lists[0].append(device_partial(rounded_x2, grad_hidden_f))
        grad_lists[1].append(device_partial(taps_f, grad_conv_f))
        grad_lists[2].append(device_partial(act_f, rounded_dx1))
        grad_lists[3].append(device_partial(values_y1.astype(jnp.bfloat16), grad_hidden_g))
        grad_lists[4].append(device_partial(taps_g, grad_conv_g))
        grad_lists[5].append(device_partial(act_g, rounded_dy2))
        rebuilt_list.append(jnp.stack((values_x1.reshape(MICRO, PIX, HALF), values_x2.reshape(MICRO, PIX, HALF)), axis=1))
        cot_list.append(jnp.stack((cot_x1.reshape(MICRO, PIX, HALF), cot_x2.reshape(MICRO, PIX, HALF)), axis=1))
        values_y1, values_y2, cot_y1, cot_y2 = values_x1, values_x2, cot_x1, cot_x2
    rebuilt = jnp.stack(rebuilt_list[::-1])
    cotangents = jnp.stack(cot_list[::-1])
    grads = [jnp.stack(entries[::-1]) for entries in grad_lists]
    return rebuilt, cotangents, grads[0], grads[1], grads[2], grads[3], grads[4], grads[5]
```

```python
import functools

import jax
import jax.numpy as jnp
from jax import lax
from jax.experimental import pallas as pl
from jax.experimental.pallas import tpu as pltpu
from jax.sharding import PartitionSpec as P

COLS = 8
LOSS_SCALE = 32.0
BF16 = jnp.bfloat16
F32 = jnp.float32


def nn(left, right):
    return jnp.dot(left, right, preferred_element_type=F32)


def nt(left, right):
    return lax.dot_general(left, right, (((1,), (1,)), ((), ())), preferred_element_type=F32)


def tn(left, right):
    return lax.dot_general(left, right, (((0,), (0,)), ((), ())), preferred_element_type=F32)


def side_shifts(values):
    length, width = values.shape
    cells = values.reshape(length // COLS, COLS, width)
    column = lax.broadcasted_iota(jnp.int32, cells.shape, 1)
    left = jnp.where(column == 0, 0.0, pltpu.roll(cells, 1, 1))
    right = jnp.where(column == COLS - 1, 0.0, pltpu.roll(cells, COLS - 1, 1))
    return [entry.reshape(length, width).astype(BF16) for entry in (left, cells, right)]


class Sizes:
    def __init__(self, micro, pixels, half, rank, peers, sections):
        self.micro, self.pixels, self.half, self.rank = micro, pixels, half, rank
        self.peers, self.sections = peers, sections
        self.rows = pixels // COLS
        assert self.rows == 4 and half == 2 * rank
        self.band = micro * COLS
        self.in_rows = half // peers
        self.core_rows = 9 * rank // peers
        self.out_rows = rank // peers
        self.piece = self.in_rows + self.core_rows + 2 * self.out_rows


def prep_kernel(sz, values, cots, *outs):
    band = sz.band
    even = lax.rem(lax.axis_index("rows"), 2) == 0

    def row(source, which, index):
        start = pl.multiple_of(index * COLS, COLS)
        parts = [source[m, which, pl.ds(start, COLS), :] for m in range(sz.micro)]
        return jnp.concatenate(parts, axis=0).astype(BF16)

    for source, major, minor, (side_a, side_b, middle) in (
        (values, 0, 1, outs[:3]),
        (cots, 1, 0, outs[3:]),
    ):
        for out, first, single in (
            (side_a, jnp.where(even, 2, 0), jnp.where(even, 3, 0)),
            (side_b, jnp.where(even, 0, 2), jnp.where(even, 0, 3)),
        ):
            out[0:band, :] = row(source, major, first)
            out[band : 2 * band, :] = row(source, major, first + 1)
            out[2 * band : 3 * band, :] = row(source, minor, single)
        middle[0:band, :] = row(source, minor, 1)
        middle[band : 2 * band, :] = row(source, minor, 2)


def prep(sz, values, cots):
    side = jax.ShapeDtypeStruct((3 * sz.band, sz.half), BF16)
    middle = jax.ShapeDtypeStruct((2 * sz.band, sz.half), BF16)
    return pl.pallas_call(
        functools.partial(prep_kernel, sz),
        out_shape=(side, side, middle) * 2,
        in_specs=[pl.BlockSpec(memory_space=pltpu.VMEM)] * 2,
        out_specs=[pl.BlockSpec(memory_space=pltpu.VMEM)] * 6,
        name="prep",
    )(values, cots)


STATE = ("rebuilt", "cotangents", "sfr", "sfw", "sbr", "sbw")


def slot_kernel(sz, plan, names_in, names_out, *refs):
    count_in, count_out = len(names_in), len(names_out)
    ins = dict(zip(names_in, refs[:count_in]))
    outs = dict(zip(names_out, refs[count_in : count_in + count_out]))
    (
        w_in_g, w_core_g, w_out_g, w_in_f, w_core_f, w_out_f,
        major, minor, slope_own, slope_a, slope_b, wide3, wide3b,
        stage, send_a, send_b, send_m, sl_a, sl_b,
        sfr, sfw, sbr, sbw, grad_core, grad_in, grad_out, sems, out_sems, small_sems,
    ) = refs[count_in + count_out :]
    band, rank, half, peers = sz.band, sz.rank, sz.half, sz.peers
    section = lax.axis_index("section")
    me = lax.axis_index("rows")
    even = lax.rem(me, 2) == 0
    fwd_on = section == plan["fwd"]
    bwd_on = section == plan["bwd"]

    def weight_copies(kind, part):
        target_in, target_core, target_out = (
            (w_in_g, w_core_g, w_out_g) if kind == "g" else (w_in_f, w_core_f, w_out_f)
        )
        base = 0 if kind == "g" else 3
        copies = []
        for j in range(peers):
            source = ins[f"{kind}{j}"]
            owner = jnp.bitwise_xor(me, j)
            if part == 0:
                where = pl.multiple_of(owner * sz.in_rows, sz.in_rows)
                copies.append((source.at[pl.ds(0, sz.in_rows), :], target_in.at[pl.ds(where, sz.in_rows), :]))
            elif part == 1:
                where = pl.multiple_of(owner * sz.core_rows, sz.core_rows)
                copies.append(
                    (source.at[pl.ds(sz.in_rows, sz.core_rows), :], target_core.at[pl.ds(where, sz.core_rows), :])
                )
            else:
                where = pl.multiple_of(owner * sz.out_rows, sz.out_rows)
                for side in range(2):
                    start = sz.in_rows + sz.core_rows + side * sz.out_rows
                    copies.append(
                        (
                            source.at[pl.ds(start, sz.out_rows), :],
                            target_out.at[pl.ds(where, sz.out_rows), pl.ds(side * rank, rank)],
                        )
                    )
        return [pltpu.make_async_copy(a, b, sems.at[base + part]) for a, b in copies]

    def weight_start(kind, part):
        for copy in weight_copies(kind, part):
            copy.start()

    def weight_wait(kind, part):
        target = {"g": (w_in_g, w_core_g, w_out_g), "f": (w_in_f, w_core_f, w_out_f)}[kind][part]
        pltpu.make_async_copy(target, target, sems.at[(0 if kind == "g" else 3) + part]).wait()

    def load_copies(prefix):
        result = []
        for index, (name, place) in enumerate((("rb", 0), ("pb", 1), ("pa", 2), ("ra", 3))):
            source = ins[prefix + name]
            spot = jnp.where(even, place, 3 - place)
            start = pl.multiple_of(spot * 2 * band, 2 * band)
            result.append((source.at[pl.ds(0, 2 * band), :], major.at[pl.ds(start, 2 * band), :]))
            line = jnp.where(even, (0, 1, 4, 5)[index], (5, 4, 1, 0)[index])
            start = pl.multiple_of(line * band, band)
            result.append((source.at[pl.ds(2 * band, band), :], minor.at[pl.ds(start, band), :]))
        result.append((ins[prefix + "pm"].at[:, :], minor.at[pl.ds(2 * band, 2 * band), :]))
        return [pltpu.make_async_copy(a, b, small_sems.at[k]) for k, (a, b) in enumerate(result)]

    def put_pieces(prime, second):
        for parity, flag in ((0, even), (1, jnp.logical_not(even))):

            @pl.when(flag)
            def _(parity=parity):
                top = (slice(0, 2 * band), slice(0, band))
                bottom = (slice(2 * band, 4 * band), slice(3 * band, 4 * band))
                for out, (pair, single) in (
                    (send_a, bottom if parity == 0 else top),
                    (send_b, top if parity == 0 else bottom),
                ):
                    out[0 : 2 * band, :] = prime[pair]
                    out[2 * band : 3 * band, :] = second[single]

        send_m[...] = second[band : 3 * band]

    def put_stage(which, values):
        for r in range(sz.rows):
            for m in range(sz.micro):
                start = (r * sz.micro + m) * COLS
                stage[m, which, r * COLS : (r + 1) * COLS, :] = values[start : start + COLS]

    def send_out(pairs):
        copies = [pltpu.make_async_copy(a, b, out_sems.at[k]) for k, (a, b) in enumerate(pairs)]
        for copy in copies:
            copy.start()
        for copy in copies:
            copy.wait()

    def gate(values):
        sigma = 1.0 / (1.0 + jnp.exp(-values))
        return values / (1.0 + jnp.exp(-values)), sigma * (1.0 + values * (1.0 - sigma))

    def conv(source, weights, rows):
        total = None
        for block in range(3):
            term = nn(source[block * band : (block + rows) * band, :], weights[block * 3 * rank : (block + 1) * 3 * rank, :])
            total = term if total is None else total + term
        return total

    def conv_back(source, weights, rows):
        total = None
        for down in range(3):
            for side in range(3):
                tap = 3 * (2 - down) + (2 - side)
                term = nt(
                    source[down * band : (down + rows) * band, side * rank : (side + 1) * rank],
                    weights[tap * rank : (tap + 1) * rank, :],
                )
                total = term if total is None else total + term
        return total

    def put_shifts(target, values, length):
        for index, entry in enumerate(side_shifts(values)):
            target[0:length, index * rank : (index + 1) * rank] = entry

    def forward():
        loads = load_copies("f_")
        for copy in loads:
            copy.start()
        for kind in ("g", "f"):
            for part in range(3):
                weight_start(kind, part)
        for copy in loads:
            copy.wait()
        weight_wait("g", 0)
        hidden = nn(major[...], w_in_g[...])
        put_shifts(wide3, hidden, 8 * band)
        sfr[0 : 4 * band, :] = wide3[2 * band : 6 * band, rank : 2 * rank]
        weight_wait("g", 1)
        act, slope = gate(conv(wide3, w_core_g, 6))
        act = act.astype(BF16)
        sfr[4 * band : 8 * band, :] = act[band : 5 * band]
        slope_own[0 : 4 * band, :] = slope[band : 5 * band]
        weight_wait("g", 2)
        second = minor[...].astype(F32) - nn(act, w_out_g[...])
        put_stage(1, second[band : 5 * band])
        second = second.astype(BF16)
        sfw[0 : 4 * band, :] = major[2 * band : 6 * band, :]
        sfw[4 * band : 8 * band, :] = second[band : 5 * band]
        weight_wait("f", 0)
        hidden = nn(second, w_in_f[...])
        line = lax.broadcasted_iota(jnp.int32, hidden.shape, 0)
        low = jnp.where(me > 0, 0, band)
        high = jnp.where(me < peers - 1, 6 * band, 5 * band)
        hidden = jnp.where((line >= low) & (line < high), hidden, 0.0)
        put_shifts(wide3b, hidden, 6 * band)
        sfr[8 * band : 12 * band, :] = wide3b[band : 5 * band, rank : 2 * rank]
        weight_wait("f", 1)
        act, slope = gate(conv(wide3b, w_core_f, 4))
        act = act.astype(BF16)
        sfr[12 * band : 16 * band, :] = act
        slope_own[4 * band : 8 * band, :] = slope
        weight_wait("f", 2)
        first = major[2 * band : 6 * band, :].astype(F32) - nn(act, w_out_f[...])
        put_stage(0, first)
        put_pieces(first.astype(BF16), sfw[4 * band : 8 * band, :])
        for parity, flag in ((0, even), (1, jnp.logical_not(even))):

            @pl.when(flag)
            def _(parity=parity):
                top = (slice(0, 2 * band), slice(4 * band, 5 * band))
                bottom = (slice(2 * band, 4 * band), slice(7 * band, 8 * band))
                for out, (pair, single) in (
                    (sl_a, bottom if parity == 0 else top),
                    (sl_b, top if parity == 0 else bottom),
                ):
                    out[0 : 2 * band, :] = slope_own[pair, :].astype(BF16)
                    out[2 * band : 3 * band, :] = slope_own[single, :].astype(BF16)

        send_out(
            [
                (send_b, outs["pb"]), (send_a, outs["pa"]), (send_m, outs["pm"]),
                (sl_a, outs["sla"]), (sl_b, outs["slb"]), (slope_own, outs["slope"]),
                (stage, outs["rebuilt"].at[0]), (sfr, outs["sfr"]), (sfw, outs["sfw"]),
            ]
        )

    def backward(last):
        loads = load_copies("b_")
        loads += [
            pltpu.make_async_copy(a, b, small_sems.at[9 + k])
            for k, (a, b) in enumerate(
                ((ins["slope"], slope_own), (ins["sra"], slope_a), (ins["srb"], slope_b))
            )
        ]
        for copy in loads:
            copy.start()
        for kind, part in (("g", 2), ("g", 1), ("g", 0), ("f", 2), ("f", 1), ("f", 0)):
            weight_start(kind, part)
        for copy in loads:
            copy.wait()
        halo_a, halo_b = slope_a[...].astype(F32), slope_b[...].astype(F32)
        above = jnp.where(even, halo_b, halo_a)
        below = jnp.where(even, halo_a, halo_b)
        weight_wait("g", 2)
        steep = jnp.concatenate([above[: 2 * band], slope_own[0 : 4 * band, :], below[: 2 * band]], axis=0)
        local = nt(major[...], w_out_g[...]) * steep
        put_shifts(wide3, local, 8 * band)
        sbr[0 : 6 * band, :] = wide3[band : 7 * band, rank : 2 * rank]
        weight_wait("g", 1)
        hidden = conv_back(wide3, w_core_g, 6).astype(BF16)
        sbr[6 * band : 10 * band, :] = hidden[band : 5 * band]
        weight_wait("g", 0)
        first = minor[...].astype(F32) + nt(hidden, w_in_g[...])
        put_stage(0, first[band : 5 * band])
        first = first.astype(BF16)
        sbw[0 : 4 * band, :] = major[2 * band : 6 * band, :]
        sbw[4 * band : 8 * band, :] = first[band : 5 * band]
        weight_wait("f", 2)
        steep = jnp.concatenate([above[2 * band :], slope_own[4 * band : 8 * band, :], below[2 * band :]], axis=0)
        local = nt(first, w_out_f[...]) * steep
        put_shifts(wide3b, local, 6 * band)
        sbr[10 * band : 16 * band, :] = wide3b[0 : 6 * band, rank : 2 * rank]
        weight_wait("f", 1)
        hidden = conv_back(wide3b, w_core_f, 4).astype(BF16)
        sbr[16 * band : 20 * band, :] = hidden
        weight_wait("f", 0)
        second = major[2 * band : 6 * band, :].astype(F32) + nt(hidden, w_in_f[...])
        put_stage(1, second)
        pairs = [(stage, outs["cotangents"].at[0])]
        if not last:
            put_pieces(second.astype(BF16), sbw[4 * band : 8 * band, :])
            pairs = [
                (send_b, outs["pb"]), (send_a, outs["pa"]), (send_m, outs["pm"]),
                (sbr, outs["sbr"]), (sbw, outs["sbw"]),
            ] + pairs
        send_out(pairs)

    def gradients(kind):
        at_f, at_w, at_b = (0, 0, 0) if kind == "g" else (8 * band, 4 * band, 10 * band)
        hidden, act = sfr[at_f : at_f + 4 * band, :], sfr[at_f + 4 * band : at_f + 8 * band, :]
        error, back = sbr[at_b : at_b + 6 * band, :], sbr[at_b + 6 * band : at_b + 10 * band, :]
        grad = tn(act, sbw[at_w : at_w + 4 * band, :]).astype(BF16)
        for side in range(2):
            grad_out[side] = grad[:, side * rank : (side + 1) * rank]
        grad_in[...] = tn(sfw[at_w : at_w + 4 * band, :], back).astype(BF16)
        left, mid, right = side_shifts(error.astype(F32))
        turned = hidden.astype(F32).T.astype(BF16)
        for down in range(3):
            for side, entry in enumerate((right, mid, left)):
                tap = 3 * down + side
                grad = nn(turned, entry[(2 - down) * band : (6 - down) * band])
                grad_core[tap * rank : (tap + 1) * rank, :] = grad.astype(BF16)
        copies = []
        for j in range(peers):
            owner = jnp.bitwise_xor(me, j)
            target = outs[kind + ("odd" if j % 2 else "even")].at[j // 2]
            start_in = pl.multiple_of(owner * sz.in_rows, sz.in_rows)
            start_core = pl.multiple_of(owner * sz.core_rows, sz.core_rows)
            start_out = pl.multiple_of(owner * sz.out_rows, sz.out_rows)
            copies.append((grad_in.at[pl.ds(start_in, sz.in_rows), :], target.at[pl.ds(0, sz.in_rows), :]))
            copies.append(
                (grad_core.at[pl.ds(start_core, sz.core_rows), :], target.at[pl.ds(sz.in_rows, sz.core_rows), :])
            )
            for side in range(2):
                spot = sz.in_rows + sz.core_rows + side * sz.out_rows
                copies.append(
                    (grad_out.at[side, pl.ds(start_out, sz.out_rows), :], target.at[pl.ds(spot, sz.out_rows), :])
                )
        index = 6 if kind == "g" else 7
        for a, b in copies:
            pltpu.make_async_copy(a, b, sems.at[index]).start()

        def finish():
            for target in (grad_in, grad_core, grad_out):
                pltpu.make_async_copy(target, target, sems.at[index]).wait()

        return finish

    if plan["fwd"] is not None and plan["fwd"] >= 0:
        pl.when(fwd_on)(forward)
    if plan["bwd"] is not None and not plan["last"]:
        pl.when(bwd_on)(functools.partial(backward, False))
    if plan["last"]:
        saves = [(ins["sfr"], sfr), (ins["sfw"], sfw)]
        copies = [pltpu.make_async_copy(a, b, small_sems.at[12 + k]) for k, (a, b) in enumerate(saves)]
        for copy in copies:
            copy.start()
        pl.when(bwd_on)(functools.partial(backward, True))

        @pl.when(jnp.logical_not(bwd_on))
        def _():
            more = [
                pltpu.make_async_copy(a, b, small_sems.at[14 + k])
                for k, (a, b) in enumerate(((ins["sbr"], sbr), (ins["sbw"], sbw)))
            ]
            for copy in more:
                copy.start()
            for copy in more:
                copy.wait()

        for copy in copies:
            copy.wait()
        gradients("g")()
        gradients("f")()


def run_slot(sz, plan, feeds, state):
    band, rank, half = sz.band, sz.rank, sz.half
    any_spec = pl.BlockSpec(memory_space=pl.ANY)
    names_in = list(feeds)
    operands = [feeds[name] for name in names_in]
    shapes = {
        "rebuilt": ((1, sz.micro, 2, sz.pixels, half), F32),
        "cotangents": ((1, sz.micro, 2, sz.pixels, half), F32),
        "sfr": ((16 * band, rank), BF16),
        "sfw": ((8 * band, half), BF16),
        "sbr": ((20 * band, rank), BF16),
        "sbw": ((8 * band, half), BF16),
        "pa": ((3 * band, half), BF16),
        "pb": ((3 * band, half), BF16),
        "pm": ((2 * band, half), BF16),
        "sla": ((3 * band, rank), BF16),
        "slb": ((3 * band, rank), BF16),
        "slope": ((8 * band, rank), F32),
        "geven": ((sz.peers // 2, sz.piece, rank), BF16),
        "godd": ((sz.peers // 2, sz.piece, rank), BF16),
        "feven": ((sz.peers // 2, sz.piece, rank), BF16),
        "fodd": ((sz.peers // 2, sz.piece, rank), BF16),
    }
    aliases = {}
    names_out = []
    for name in STATE:
        if state is None:
            names_out.append(name)
        elif not (plan["last"] and name != "cotangents"):
            aliases[len(operands)] = len(names_out)
            names_in.append(name)
            operands.append(state[name])
            names_out.append(name)
        elif name != "rebuilt":
            names_in.append(name)
            operands.append(state[name])
    if plan["last"]:
        names_out += ["geven", "godd", "feven", "fodd"]
    else:
        names_out += ["pa", "pb", "pm"]
        if plan["fwd"] is not None:
            names_out += ["sla", "slb", "slope"]
    scratch = [
        pltpu.VMEM((half, rank), BF16), pltpu.VMEM((9 * rank, rank), BF16), pltpu.VMEM((rank, half), BF16),
        pltpu.VMEM((half, rank), BF16), pltpu.VMEM((9 * rank, rank), BF16), pltpu.VMEM((rank, half), BF16),
        pltpu.VMEM((8 * band, half), BF16), pltpu.VMEM((6 * band, half), BF16),
        pltpu.VMEM((8 * band, rank), F32), pltpu.VMEM((3 * band, rank), BF16), pltpu.VMEM((3 * band, rank), BF16),
        pltpu.VMEM((8 * band, 3 * rank), BF16), pltpu.VMEM((6 * band, 3 * rank), BF16),
        pltpu.VMEM((sz.micro, 2, sz.pixels, half), F32),
        pltpu.VMEM((3 * band, half), BF16), pltpu.VMEM((3 * band, half), BF16), pltpu.VMEM((2 * band, half), BF16),
        pltpu.VMEM((3 * band, rank), BF16), pltpu.VMEM((3 * band, rank), BF16),
        pltpu.VMEM((16 * band, rank), BF16), pltpu.VMEM((8 * band, half), BF16),
        pltpu.VMEM((20 * band, rank), BF16), pltpu.VMEM((8 * band, half), BF16),
        pltpu.VMEM((9 * rank, rank), BF16), pltpu.VMEM((half, rank), BF16), pltpu.VMEM((2, rank, rank), BF16),
        pltpu.SemaphoreType.DMA((8,)), pltpu.SemaphoreType.DMA((9,)), pltpu.SemaphoreType.DMA((16,)),
    ]
    results = pl.pallas_call(
        functools.partial(slot_kernel, sz, plan, names_in, names_out),
        out_shape=[jax.ShapeDtypeStruct(*shapes[name]) for name in names_out],
        in_specs=[any_spec] * len(operands),
        out_specs=[any_spec] * len(names_out),
        scratch_shapes=scratch,
        input_output_aliases=aliases,
        compiler_params=pltpu.CompilerParams(has_side_effects=True, vmem_limit_bytes=40 * 2**20),
        cost_estimate=pl.CostEstimate(flops=2 * 10**9, bytes_accessed=6 * 10**6, transcendentals=10**5),
        name=plan["name"],
    )(*operands)
    return dict(zip(names_out, results))


def swap_near(values, peers):
    return lax.ppermute(values, "rows", [(i, i ^ 1) for i in range(peers)])


def swap_far(values, peers):
    pairs = [(i, i + 1) for i in range(1, peers - 1, 2)]
    return lax.ppermute(values, "rows", pairs + [(j, i) for i, j in pairs])


def flip(values, bit, peers):
    return lax.ppermute(values, "rows", [(i, i ^ (1 << bit)) for i in range(peers)])


def gather(piece, order, peers):
    held = {0: piece}
    for bit in order:
        held.update({j | (1 << bit): flip(value, bit, peers) for j, value in sorted(held.items())})
    return [held[j] for j in range(peers)]


def scatter(kept, sent, order, peers):
    got = flip(sent, 0, peers)
    totals = {2 * k: kept[k].astype(F32) + got[k].astype(F32) for k in range(peers // 2)}
    for bit in order:
        mask = 1 << bit
        later = [j for j in totals if j & mask]
        arrived = {j ^ mask: flip(totals[j].astype(BF16), bit, peers) for j in sorted(later, reverse=True)}
        totals = {j: totals[j] + value.astype(F32) for j, value in arrived.items()}
    return totals[0] / LOSS_SCALE


def shards(top_values, top_cotangents, f_input, f_kernel, f_output, g_input, g_kernel, g_output):
    sections, peers = lax.axis_size("section"), lax.axis_size("rows")
    rank = f_input.shape[2]
    sz = Sizes(top_values.shape[0], top_values.shape[2], top_values.shape[3], rank, peers, sections)
    bits = peers.bit_length() - 1
    assert peers == 1 << bits

    def pack(w_in, w_core, w_out):
        return jnp.concatenate([w_in[0], w_core[0], w_out[0][:, :rank], w_out[0][:, rank:]], axis=0)

    upward = list(range(1, bits))
    pieces = {}
    for kind, arrays, order in (
        ("g", (g_input, g_kernel, g_output), upward + [0]),
        ("f", (f_input, f_kernel, f_output), upward[::-1] + [0]),
    ):
        for j, value in enumerate(gather(pack(*arrays), order, peers)):
            pieces[f"{kind}{j}"] = value
    prepared = prep(sz, top_values, top_cotangents)
    names = ("pa", "pb", "pm")
    fresh = dict(zip(names, prepared[:3]))
    cots = dict(zip(names, prepared[3:]))
    for group in (fresh, cots):
        group["rb"] = swap_far(group["pb"], peers)
        group["ra"] = swap_near(group["pa"], peers)
    state, slopes = None, None
    for slot in range(sections + 1):
        last = slot == sections
        plan = {
            "fwd": None if last else sections - 1 - slot,
            "bwd": sections - slot if slot else None,
            "last": last,
            "name": f"slot{slot}",
        }
        feeds = dict(pieces)
        if not last:
            feeds.update({"f_" + name: value for name, value in fresh.items()})
        if slot:
            feeds.update({"b_" + name: value for name, value in (cots if slot == 1 else fresh).items()})
            feeds.update(slopes)
        result = run_slot(sz, plan, feeds, state)
        if last:
            break
        state = {name: result[name] for name in STATE}
        hops = [(s, s - 1) for s in (plan["fwd"], plan["bwd"]) if s is not None and s >= 1]
        fresh = {name: lax.ppermute(result[name], "section", hops) for name in ("pb", "pa", "pm")}
        fresh["rb"] = swap_far(fresh["pb"], peers)
        fresh["ra"] = swap_near(fresh["pa"], peers)
        slopes = {
            "slope": result["slope"],
            "sra": swap_near(result["sla"], peers),
            "srb": swap_far(result["slb"], peers),
        }
    grads = {}
    for kind, order in (("g", upward), ("f", upward[::-1])):
        total = scatter(result[kind + "even"], result[kind + "odd"], order, peers)
        split = sz.in_rows + sz.core_rows
        grads[kind] = (
            total[None, : sz.in_rows],
            total[None, sz.in_rows : split],
            jnp.concatenate([total[split : split + sz.out_rows], total[split + sz.out_rows :]], axis=1)[None],
        )
    return (state["rebuilt"], result["cotangents"]) + grads["f"] + grads["g"]


def solution(mesh):
    return jax.shard_map(
        shards,
        mesh=mesh,
        in_specs=(P(None, None, "rows", None),) * 2 + (P("section", "rows", None),) * 6,
        out_specs=(P("section", None, None, "rows", None),) * 2 + (P("section", "rows", None),) * 6,
        check_vma=False,
    )
```
